32 devices in a mesh: expert: 4 (over x, core), tensor: 4 (over z), kv: 2 (over y).
Axes of the slice: x: 2, y: 2, z: 4, core: 2. Of those that a mesh axis runs over, the one named last changes fastest.
Arguments:
- residual_stream: bfloat16 [1024, 4096], P('expert', ('tensor', 'kv')), may hold values from -13 to 13
- grad_output: bfloat16 [1024, 4096], P('expert', ('tensor', 'kv')), may hold values from -6 to 6
- norm_gain: bfloat16 [4096], P(('tensor', 'kv')), may hold values from 0.5 to 1.5
- expert_ids: int32 [1024, 2], P('expert'), may hold values from 0 to 3, all different within a row; in each aligned block of 256 rows (0 to 255, 256 to 511, ...) at most 160 rows name the same one
- gate_probs: float32 [1024, 2], P('expert'), may hold values from 0.1 to 0.9
- w_gate: bfloat16 [4, 14336, 4096], P('expert', ('tensor', 'kv')), may hold values from -0.125 to 0.125
- w_up: bfloat16 [4, 14336, 4096], P('expert', ('tensor', 'kv')), may hold values from -0.125 to 0.125
- w_down: bfloat16 [4, 14336, 4096], P('expert', ('tensor', 'kv')), may hold values from -0.046875 to 0.046875
Outputs:
- input_grad: bfloat16 [1024, 4096], P('expert', ('tensor', 'kv'))
The draws below stay inside these ranges and needn't reach their ends.
Inputs may be any that keep to these rules, and one draw needn't show every extreme that they name: `expert_ids`: each row names two different experts. In each aligned block of 256 rows (the rows of one index of the expert axis) no expert is named by more than 160 rows, a bound that some block reaches.
All inputs are finite; a program needn't handle non-finite values.
Results may differ from the reference program's by a relative error of at most 0.018.
Values may be sent and summed in bfloat16 or wider, within the bound.
A program may use at most 128 MiB of HBM per device.

```python
import math
import jax
import jax.numpy as jnp
import numpy as np
from jax import lax

D = 4096
FF = 14336
TOK_DEV = 256
CAP = 160
EXPERTS = 4
TOKENS = 1024
N_EXPERT = 4


def draw_residual_stream(key, part):
    keys = jax.random.split(jax.random.fold_in(key, 17), 3)
    row_scale = 10.0 ** jax.random.uniform(keys[0], (TOKENS, 1), jnp.float32, -1.5, -0.5)
    ramp = jnp.arange(D, dtype=jnp.float32)[None, :] / D
    col_scale = 10.0 ** (0.5 * ramp + 0.5 * jax.random.uniform(keys[1], (1, D), jnp.float32))
    base = jax.random.normal(keys[2], (TOKENS, D), jnp.float32)
    base = jnp.clip(base, -4.0, 4.0)
    return (base * row_scale * col_scale).astype(jnp.bfloat16)


def with_spikes(drawn, own_key, source, target, blocks, factor):
    owner, partner = [(jnp.arange(drawn.shape[dim]) // (drawn.shape[dim] // blocks)).reshape([-1 if axis == dim else 1 for axis in range(drawn.ndim)]) for dim in (source, target)]
    chosen = jax.random.permutation(own_key, blocks)[partner]
    strong = (owner == chosen) | (owner == (partner + blocks // 2) % blocks)
    return jnp.where(strong, factor * drawn, drawn)


def shard_levels(own_key, dims, cuts, low, top_value):
    factor_of, own = 1.0, jax.random.fold_in(own_key, 6)
    for axis_at, blocks in cuts:
        heights = jnp.exp(jax.random.uniform(jax.random.fold_in(own, axis_at), (blocks,), jnp.float32, low / len(cuts), top_value / len(cuts)))
        factor_of = factor_of * jnp.repeat(heights, dims[axis_at] // blocks).reshape([-1 if axis == axis_at else 1 for axis in range(len(dims))])
    return factor_of


def routed_block(stream_key, own, number, rows, amount, top, bound, skew):
    order = jax.random.permutation(stream_key, amount)
    packed, usual = portions_of(amount, rows * top, bound, skew, True), portions_of(amount, rows * top, bound, skew, False)
    places = jnp.arange(amount)

    def named(tallies, rotation):
        used = int((tallies > 0).sum())
        fixed = max(1, used // 4)
        moved = fixed + (places - fixed + rotation * (used - fixed)) % max(1, amount - fixed)
        return jnp.zeros((amount,), jnp.int32).at[order[jnp.where(places < fixed, places, moved)]].set(jnp.asarray(tallies, jnp.int32))

    tallies = jnp.where(number % 4 == 0, named(packed, number // 4), named(usual, number - number // 4 - 1))
    mixed = jax.random.permutation(jax.random.fold_in(own, 3), amount)
    donor, taker = mixed[0:amount // 2 * 2:2], mixed[1:amount // 2 * 2:2]
    slack = jnp.minimum(tallies[donor] - 1, bound - tallies[taker]) // 2
    slack = jnp.where((donor == order[0]) | (taker == order[0]) | (tallies[taker] == 0), 0, jnp.maximum(slack, 0))
    moved = jax.random.randint(jax.random.fold_in(own, 4), (amount // 2,), 0, 1 << 20) % (slack + 1)
    tallies = tallies.at[donor].add(-moved).at[taker].add(moved)
    items = jnp.searchsorted(jnp.cumsum(tallies), jnp.arange(rows * top), side="right").astype(jnp.int32)
    table = items.reshape(top, rows).T
    table = table[jax.random.permutation(jax.random.fold_in(own, 1), rows)]
    rotation = jax.random.randint(jax.random.fold_in(own, 2), (rows, 1), 0, top)
    return jnp.take_along_axis(table, (jnp.arange(top)[None, :] + rotation) % top, axis=1)


def portions_of(amount, total, bound, lean, full):
    loads = [(1 << 20) // math.isqrt(standing ** lean) + 1 for standing in range(1, amount + 1)]
    largest = bound if full else min(bound, max(-(-total // amount), total * loads[0] // sum(loads)))
    least = 1 if total - largest >= amount - 1 else 0
    counts, rest = [largest] + [least] * (amount - 1), total - largest - least * (amount - 1)
    while rest > 0:
        movable = [i for i in range(1, amount) if counts[i] < largest] or [i for i in range(1, amount) if counts[i] < bound]
        whole, remaining = sum([loads[i] for i in movable]), rest
        for i in movable:
            addition = min(bound - counts[i], max(1, remaining * loads[i] // whole), rest)
            counts[i] = counts[i] + addition
            rest = rest - addition
    return np.array(counts)


def centred(own_key, dims, width, limit, cuts=(), kind=jnp.bfloat16):
    factor_of = shard_levels(own_key, dims, cuts, -0.22, 0.18) if cuts else 1.0
    drawn = jax.random.normal(own_key, dims, jnp.float32) * width * factor_of
    return jnp.minimum(jnp.maximum(drawn, -limit), limit).astype(kind)


def bell_draw_with(stream_key, shape, scale, most, cuts, heavy, kind=jnp.bfloat16):
    values = scale * jax.random.normal(stream_key, shape, jnp.float32)
    if cuts:
        values = values * shard_levels(stream_key, shape, cuts, -0.22, 0.18)
    return jnp.clip(with_spikes(values, jax.random.fold_in(stream_key, 3), *heavy), -most, most).astype(kind)


def setup_inputs(seed: int = 0) -> dict:
    seeds = jax.random.split(jax.random.key(seed), 9)
    residual_stream = draw_residual_stream(jax.random.fold_in(seeds[8], 71), 0)
    grad_output = centred(seeds[1], (TOKENS, D), 1.0, 6.0, ((0, 4), (1, 8)))
    norm_gain = jnp.clip(1.0 + 0.1 * jax.random.normal(seeds[2], (D,), jnp.float32), 0.5, 1.5).astype(jnp.bfloat16)
    expert_ids_keys = jax.random.split(jax.random.fold_in(seeds[3], 1), TOKENS // TOK_DEV)
    expert_ids_turns = jax.random.permutation(jax.random.fold_in(seeds[3], 3), TOKENS // TOK_DEV)
    expert_ids = jax.vmap(lambda own, number: routed_block(jax.random.fold_in(seeds[3], 2), own, number, TOK_DEV, EXPERTS, 2, CAP, 2))(expert_ids_keys, expert_ids_turns).reshape((TOKENS, 2))
    gate_probs = jnp.clip(0.1 + 0.79999997 * jax.random.uniform(seeds[4], (TOKENS, 2), jnp.float32) ** shard_levels(seeds[4], (TOKENS, 2), ((0, 4),), -0.2, 0.2), 0.1, 0.9)
    w_gate = bell_draw_with(seeds[5], (EXPERTS, FF, D), D ** -0.5, 0.125, ((0, 4), (1, 8)), (1, 2, 8, 2.0))
    w_up = bell_draw_with(seeds[6], (EXPERTS, FF, D), D ** -0.5, 0.125, ((0, 4), (1, 8)), (1, 2, 8, 2.0))
    w_down = centred(seeds[7], (EXPERTS, FF, D), FF ** -0.5, 0.046875, ((0, 4), (1, 8)))
    return dict(residual_stream=residual_stream, grad_output=grad_output, norm_gain=norm_gain, expert_ids=expert_ids, gate_probs=gate_probs, w_gate=w_gate, w_up=w_up, w_down=w_down)


epsilon = 1e-05
contract_width = (((1,), (1,)), ((), ()))

def slot_matrix(ids_block, experts):
    flattened = ids_block.reshape(-1)
    onehot = (flattened[:, None] == jnp.arange(experts, dtype=jnp.int32)[None, :]).astype(jnp.int32)
    before = jnp.cumsum(onehot, axis=0) - onehot
    position = lax.optimization_barrier(jnp.sum(before * onehot, axis=1))
    slot_index = flattened * CAP + position
    table = jnp.arange(experts * CAP, dtype=jnp.int32)
    return (slot_index[None, :] == table[:, None]).astype(jnp.bfloat16)

def dispatch_block(ids_block, normed_block, grad_block, prob_block):
    table = slot_matrix(ids_block, EXPERTS)
    repeated_x = jnp.repeat(normed_block, 2, axis=0)
    scaled = (jnp.repeat(grad_block.astype(jnp.float32), 2, axis=0) * prob_block.reshape(-1, 1)).astype(jnp.bfloat16)
    routed_x = jnp.dot(table, repeated_x, preferred_element_type=jnp.float32).astype(jnp.bfloat16)
    routed_grad = jnp.dot(table, scaled, preferred_element_type=jnp.float32).astype(jnp.bfloat16)
    return (table, routed_x, routed_grad)

def expert_grad(operands):
    routed_x, routed_grad, gate_weight, up_weight, down_weight = operands
    gate_value = lax.dot_general(routed_x, gate_weight, contract_width, preferred_element_type=jnp.float32)
    up_value = lax.dot_general(routed_x, up_weight, contract_width, preferred_element_type=jnp.float32)
    act_grad = lax.dot_general(routed_grad, down_weight, contract_width, preferred_element_type=jnp.float32)
    sigmoid_gate = jax.nn.sigmoid(gate_value)
    activated = gate_value * sigmoid_gate
    gate_grad = (act_grad * up_value * sigmoid_gate * (1.0 + gate_value * (1.0 - sigmoid_gate))).astype(jnp.bfloat16)
    up_grad = (act_grad * activated).astype(jnp.bfloat16)
    slot_grad = jnp.dot(gate_grad, gate_weight, preferred_element_type=jnp.float32)
    slot_grad = slot_grad + jnp.dot(up_grad, up_weight, preferred_element_type=jnp.float32)
    return slot_grad.astype(jnp.bfloat16)

def combine_block(table, values):
    summed = lax.dot_general(table, values, (((0,), (0,)), ((), ())), preferred_element_type=jnp.float32)
    return summed.reshape(TOK_DEV, 2, D).sum(axis=1)

def reference(residual_stream, grad_output, norm_gain, expert_ids, gate_probs, w_gate, w_up, w_down):
    stream = residual_stream.astype(jnp.float32)
    squares = lax.optimization_barrier(jnp.sum(stream * stream, axis=1, keepdims=True))
    inverse_rms = lax.rsqrt(squares / D + epsilon)
    gains = norm_gain.astype(jnp.float32)
    normed = (stream * inverse_rms * gains).astype(jnp.bfloat16)
    blocks = N_EXPERT
    tables, routed_x, routed_grad = jax.vmap(dispatch_block)(expert_ids.reshape(blocks, TOK_DEV, 2), normed.reshape(blocks, TOK_DEV, D), grad_output.reshape(blocks, TOK_DEV, D), gate_probs.reshape(blocks, TOK_DEV, 2))
    expert_x = routed_x.reshape(blocks, EXPERTS, CAP, D).transpose(1, 0, 2, 3).reshape(EXPERTS, blocks * CAP, D)
    expert_dy = routed_grad.reshape(blocks, EXPERTS, CAP, D).transpose(1, 0, 2, 3).reshape(EXPERTS, blocks * CAP, D)
    expert_out = lax.map(expert_grad, (expert_x, expert_dy, w_gate, w_up, w_down))
    returned = expert_out.reshape(EXPERTS, blocks, CAP, D).transpose(1, 0, 2, 3).reshape(blocks, EXPERTS * CAP, D)
    token_grad = jax.vmap(combine_block)(tables, returned).reshape(TOKENS, D)
    scaled_grad = token_grad * gains
    projection = lax.optimization_barrier(jnp.sum(scaled_grad * stream, axis=1, keepdims=True))
    result = inverse_rms * scaled_grad - stream * inverse_rms ** 3 * projection / D
    return result.astype(jnp.bfloat16)
```

```python
import functools

import jax
import jax.numpy as jnp
from jax import lax
from jax.experimental import pallas as pl
from jax.experimental.pallas import tpu as pltpu
from jax.sharding import PartitionSpec as P

D = 4096
CAP = 160


epsilon = 1e-05
contract_width = (((1,), (1,)), ((), ()))
contract_hidden = (((0,), (1,)), ((), ()))
contract_slots = (((0,), (0,)), ((), ()))


def slot_matrix(ids_block, experts):
    flattened = ids_block.reshape(-1)
    onehot = (flattened[:, None] == jnp.arange(experts, dtype=jnp.int32)[None, :]).astype(jnp.int32)
    before = jnp.cumsum(onehot, axis=0) - onehot
    position = jnp.sum(before * onehot, axis=1)
    slot_index = flattened * CAP + position
    table = jnp.arange(experts * CAP, dtype=jnp.int32)
    return (slot_index[None, :] == table[:, None]).astype(jnp.bfloat16)


def shards(residual_stream, grad_output, norm_gain, expert_ids, gate_probs, w_gate, w_up, w_down):
    experts = lax.axis_size("expert")
    local_width = residual_stream.shape[1]
    tokens_here = residual_stream.shape[0]
    stream = residual_stream.astype(jnp.float32)
    squares = lax.psum(jnp.sum(stream * stream, axis=1), ("tensor", "kv"))
    inverse_rms = lax.rsqrt(squares / D + epsilon)[:, None]
    gains = norm_gain.astype(jnp.float32)
    normed = (stream * inverse_rms * gains).astype(jnp.bfloat16)
    table = slot_matrix(expert_ids, experts)
    repeated_x = jnp.repeat(normed, 2, axis=0)
    scaled = (
        jnp.repeat(grad_output.astype(jnp.float32), 2, axis=0) * gate_probs.reshape(-1, 1)
    ).astype(jnp.bfloat16)
    routed_x = jnp.dot(table, repeated_x, preferred_element_type=jnp.float32).astype(jnp.bfloat16)
    routed_grad = jnp.dot(table, scaled, preferred_element_type=jnp.float32).astype(jnp.bfloat16)
    routed_x = routed_x.reshape(experts, CAP, local_width)
    routed_grad = routed_grad.reshape(experts, CAP, local_width)
    gate_weight, up_weight, down_weight = (w_gate[0], w_up[0], w_down[0])
    pieces_x = lax.all_to_all(routed_x, "expert", split_axis=0, concat_axis=0, tiled=True)
    pieces_dy = lax.all_to_all(routed_grad, "expert", split_axis=0, concat_axis=0, tiled=True)
    full_x = lax.all_gather(pieces_x, ("tensor", "kv"), axis=2, tiled=True)
    full_dy = lax.all_gather(pieces_dy, ("tensor", "kv"), axis=2, tiled=True)
    leading = full_x.shape[0]
    items = full_x.shape[1]
    matrix_x = full_x.reshape(leading * items, D)
    matrix_dy = full_dy.reshape(leading * items, D)
    gate_value = lax.dot_general(
        matrix_x, gate_weight, contract_width, preferred_element_type=jnp.float32
    )
    up_value = lax.dot_general(
        matrix_x, up_weight, contract_width, preferred_element_type=jnp.float32
    )
    act_grad = lax.dot_general(
        matrix_dy, down_weight, contract_width, preferred_element_type=jnp.float32
    )
    sigmoid_gate = jax.nn.sigmoid(gate_value)
    activated = gate_value * sigmoid_gate
    gate_grad = (
        act_grad * up_value * sigmoid_gate * (1.0 + gate_value * (1.0 - sigmoid_gate))
    ).astype(jnp.bfloat16)
    up_grad = (act_grad * activated).astype(jnp.bfloat16)
    total = lax.dot_general(
        gate_weight, gate_grad, contract_hidden, preferred_element_type=jnp.float32
    )
    summed = lax.psum_scatter(
        total
        + lax.dot_general(up_weight, up_grad, contract_hidden, preferred_element_type=jnp.float32),
        ("tensor", "kv"),
        scatter_dimension=0,
        tiled=True,
    )
    returned = summed.T.astype(jnp.bfloat16).reshape(leading, items, local_width)
    combined = lax.all_to_all(returned, "expert", split_axis=0, concat_axis=0, tiled=True)
    gathered = lax.dot_general(
        table,
        combined.reshape(experts * CAP, local_width),
        contract_slots,
        preferred_element_type=jnp.float32,
    )
    token_grad = gathered.reshape(tokens_here, 2, local_width).sum(axis=1)
    scaled_grad = token_grad * gains
    projection = lax.psum(jnp.sum(scaled_grad * stream, axis=1), ("tensor", "kv"))[:, None]
    result = inverse_rms * scaled_grad - stream * inverse_rms**3 * projection / D
    return result.astype(jnp.bfloat16)


MESH = pl.DeviceIdType.MESH
TILE = 256


def fused_kernel(
    T, x_ref, dy_ref, gain_ref, meta_ref, wg_ref, wu_ref, wd_ref, out_ref,
    tok, acc, wbuf, hid, routed, crecv, xrecv, yrecv, zrecv, gains, metas, sel, prob,
    ssq, own_sq, psend, precv,
    ag_send, ag_recv, rs_send, rs_recv, small_send, small_recv, wsem, lsem,
):
    e = lax.axis_index("expert")
    z = lax.axis_index("tensor")
    y = lax.axis_index("kv")
    core = e + 1 - 2 * lax.rem(e, 2)
    across = lax.rem(e + 2, 4)
    width = x_ref.shape[1]
    hidden = wg_ref.shape[0]
    tiles = hidden // TILE
    blocks = 2 * T
    inputs = (x_ref, dy_ref)

    def z_of(d):
        return lax.rem(z + T - d, T)

    def y_of(s):
        return y if s == 0 else 1 - y

    def fb_of(d, s):
        return z_of(d) * 2 + y_of(s)

    def b_of(u, c):
        base = core if c else e
        return lax.rem(base + 2 * u, 4)

    def slot(a, d, s, u, c):
        return tok.at[a, fb_of(d, s), b_of(u, c)]

    def number(a, d, s, u, c):
        return (((a * T + d) * 2 + s) * 2 + u) * 2 + c

    def plan(a, d, s, u, c):
        if c:
            return (d, s, u, 0), (core, z, y)
        if a == 0:
            if u:
                return (d, s, 0, 0), (across, z, y)
            if s:
                return (d, 0, 0, 0), (e, z, 1 - y)
        else:
            if s:
                return (d, 0, u, 0), (e, z, 1 - y)
            if u:
                return (d, 0, 0, 0), (across, z, y)
        return (0, 0, 0, 0), (e, lax.rem(z + d, T), y)

    def gather_copy(a, d, s, u, c):
        source, target = plan(a, d, s, u, c)
        n = number(a, d, s, u, c)
        fb, b = fb_of(*source[:2]), b_of(*source[2:])
        src = inputs[a] if source == (0, 0, 0, 0) else tok.at[a, fb, b]
        return pltpu.make_async_remote_copy(
            src_ref=src, dst_ref=tok.at[a, fb, b],
            send_sem=ag_send.at[n], recv_sem=ag_recv.at[n],
            device_id=target, device_id_type=MESH,
        )

    def gather_wait(a, d, s, u, c):
        n = number(a, d, s, u, c)
        here = slot(a, d, s, u, c)
        pltpu.make_async_remote_copy(
            src_ref=here, dst_ref=here, send_sem=ag_send.at[n], recv_sem=ag_recv.at[n],
            device_id=plan(a, d, s, u, c)[1], device_id_type=MESH,
        ).wait_recv()

    steps = [(d, s) for d in range(T) for s in (0, 1)]
    back = [(d, s) for d in list(range(1, T)) + [0] for s in (1, 0)]

    def weight_copies(step):
        if step < blocks:
            fb, refs = fb_of(*steps[step]), (wg_ref, wu_ref, wd_ref)
        else:
            fb, refs = fb_of(*back[step - blocks]), (wg_ref, wu_ref)
        columns = pl.ds(pl.multiple_of(fb * width, width), width)
        return [
            pltpu.make_async_copy(ref.at[:, columns], wbuf.at[step % 2, k], wsem.at[step % 2, k])
            for k, ref in enumerate(refs)
        ]

    for copy in weight_copies(0):
        copy.start()
    local = [
        pltpu.make_async_copy(x_ref, tok.at[0, fb_of(0, 0), e], lsem.at[0]),
        pltpu.make_async_copy(dy_ref, tok.at[1, fb_of(0, 0), e], lsem.at[1]),
        pltpu.make_async_copy(gain_ref, gains.at[fb_of(0, 0)], lsem.at[2]),
        pltpu.make_async_copy(meta_ref, metas.at[e], lsem.at[3]),
    ]
    for copy in local:
        copy.start()

    peers = [(e, lax.rem(z + d, T), y_of(s)) for d in range(T) for s in (0, 1) if d or s]
    sources = [fb_of(d, s) for d in range(T) for s in (0, 1) if d or s]
    others = [(lax.rem(e + k, 4), z, y) for k in (1, 2, 3)]
    barrier = pltpu.get_barrier_semaphore()
    for peer in peers + others:
        pl.semaphore_signal(barrier, inc=1, device_id=peer, device_id_type=MESH)
    pl.semaphore_wait(barrier, len(peers) + len(others))

    def remote(src, dst, send, recv, peer):
        return pltpu.make_async_remote_copy(
            src_ref=src, dst_ref=dst, send_sem=send, recv_sem=recv,
            device_id=peer, device_id_type=MESH,
        )

    small = []
    for k, peer in enumerate(others):
        copy = remote(meta_ref, metas.at[e], small_send.at[k], small_recv.at[k], peer)
        copy.start()
        there = metas.at[lax.rem(e + 3 - k, 4)]
        small.append((copy, remote(there, there, small_send.at[k], small_recv.at[k], peer)))
    for d in range(1, T):
        for a in (0, 1):
            gather_copy(a, d, 0, 0, 0).start()
    for k, peer in enumerate(peers):
        n = 3 + k
        copy = remote(gain_ref, gains.at[fb_of(0, 0)], small_send.at[n], small_recv.at[n], peer)
        copy.start()
        there = gains.at[sources[k]]
        small.append((copy, remote(there, there, small_send.at[n], small_recv.at[n], peer)))

    def level1(d):
        if d:
            gather_wait(0, d, 0, 0, 0)
        gather_copy(0, d, 1, 0, 0).start()
        gather_copy(0, d, 0, 1, 0).start()
        gather_copy(0, d, 0, 0, 1).start()
        if d:
            gather_wait(1, d, 0, 0, 0)
        gather_copy(1, d, 0, 1, 0).start()
        gather_copy(1, d, 1, 0, 0).start()
        gather_copy(1, d, 0, 0, 1).start()

    def level2(d):
        gather_wait(0, d, 1, 0, 0)
        gather_copy(0, d, 1, 1, 0).start()
        gather_copy(0, d, 1, 0, 1).start()
        gather_wait(1, d, 0, 1, 0)
        gather_copy(1, d, 1, 1, 0).start()
        gather_copy(1, d, 0, 1, 1).start()

    def level3(d):
        gather_wait(0, d, 0, 1, 0)
        gather_copy(0, d, 0, 1, 1).start()
        gather_wait(1, d, 1, 0, 0)
        gather_copy(1, d, 1, 0, 1).start()
        gather_wait(0, d, 1, 1, 0)
        gather_copy(0, d, 1, 1, 1).start()
        gather_wait(1, d, 1, 1, 0)
        gather_copy(1, d, 1, 1, 1).start()

    def multiply(step):
        d, s = steps[step]
        for copy in weight_copies(step + 1):
            copy.start()
        for a in (0, 1):
            for u in (0, 1):
                gather_wait(a, d, s, u, 1)
        fb = fb_of(d, s)
        gain_row = gains[fb, 0:1, :]
        mine = tok[0, fb, e].astype(jnp.float32)
        own_sq[...] += jnp.sum(mine * mine, axis=1, keepdims=True)
        for b in range(4):
            rows = pl.ds(b * CAP, CAP)
            picked = jnp.dot(sel[b], tok[0, fb, b], preferred_element_type=jnp.float32)
            ssq[rows, :] += jnp.sum(picked * picked, axis=1, keepdims=True)
            routed[0, rows, :] = (picked * gain_row).astype(jnp.bfloat16)
            picked = jnp.dot(sel[b], tok[1, fb, b], preferred_element_type=jnp.float32)
            routed[1, rows, :] = (picked * prob[rows, :]).astype(jnp.bfloat16)
        for copy in weight_copies(step):
            copy.wait()

        def tile(n, carry):
            rows = pl.ds(pl.multiple_of(n * TILE, TILE), TILE)
            for k in range(3):
                term = lax.dot_general(
                    routed[k // 2], wbuf[step % 2, k, rows, :], contract_width,
                    preferred_element_type=jnp.float32,
                )
                if step == 0:
                    acc[k, n] = term
                else:
                    acc[k, n] += term
            return carry

        lax.fori_loop(0, tiles, tile, 0)

    level1(0)
    for copy in local:
        copy.wait()
    for copy, arrival in small[:3]:
        arrival.wait_recv()
    own_sq[...] = jnp.zeros_like(own_sq)
    ssq[...] = jnp.zeros_like(ssq)
    for b in range(4):
        slots = metas[b, pl.ds(e, 1), :]
        probs = metas[b, pl.ds(4 + e, 1), :]
        index = lax.broadcasted_iota(jnp.int32, (CAP, slots.shape[1]), 0).astype(jnp.float32)
        chosen = jnp.where(index == slots, 1.0, 0.0)
        sel[b] = chosen.astype(jnp.bfloat16)
        prob[pl.ds(b * CAP, CAP), :] = jnp.sum(chosen * probs, axis=1, keepdims=True)
    for copy, arrival in small[3:]:
        arrival.wait_recv()
    level1(1)
    level2(0)
    level1(2)
    level3(0)
    level2(1)
    level1(3)
    multiply(0)
    level3(1)
    level2(2)
    multiply(1)
    level2(3)
    level3(2)
    multiply(2)
    multiply(3)
    level3(3)
    for step in range(4, blocks):
        multiply(step)
    for a in (0, 1):
        for n in range(1, blocks * 4):
            c, u, s, d = n % 2, n // 2 % 2, n // 4 % 2, n // 8
            gather_copy(a, d, s, u, c).wait_send()
    for copy, arrival in small:
        copy.wait_send()

    inverse = lax.rsqrt(ssq[...] / D + epsilon)

    def activate(n, carry):
        columns = pl.ds(pl.multiple_of(n * TILE, TILE), TILE)
        gate_value = acc[0, n] * inverse
        up_value = acc[1, n] * inverse
        act_grad = acc[2, n]
        sigmoid_gate = jax.nn.sigmoid(gate_value)
        hid[0, :, columns] = (
            act_grad * up_value * sigmoid_gate * (1.0 + gate_value * (1.0 - sigmoid_gate))
        ).astype(jnp.bfloat16)
        hid[1, :, columns] = (act_grad * gate_value * sigmoid_gate).astype(jnp.bfloat16)
        return carry

    lax.fori_loop(0, tiles, activate, 0)

    def core_copy(i, u):
        return remote(
            tok.at[0, i, lax.rem(core + 2 * u, 4)], crecv.at[i, u],
            rs_send.at[i, u], rs_recv.at[i, u], (core, z, y),
        )

    def across_copy(i):
        return remote(tok.at[1, i, 0], xrecv.at[i], rs_send.at[i, 2], rs_recv.at[i, 2], (across, z, y))

    def pair_copy(i):
        d = back[i][0]
        return remote(tok.at[1, i, 1], yrecv.at[d], rs_send.at[i, 3], rs_recv.at[i, 3], (e, z, 1 - y))

    def line_copy(i):
        d = back[i][0]
        return remote(
            tok.at[1, i, 2], zrecv.at[d - 1], rs_send.at[i, 4], rs_recv.at[i, 4], (e, z_of(d), y)
        )

    def produce(i):
        step = blocks + i
        if i + 1 < blocks:
            for copy in weight_copies(step + 1):
                copy.start()
        for copy in weight_copies(step):
            copy.wait()

        def tile(n, carry):
            columns = pl.ds(pl.multiple_of(n * TILE, TILE), TILE)
            total = jnp.dot(
                hid[0], wbuf[step % 2, 0, :, columns], preferred_element_type=jnp.float32
            ) + jnp.dot(hid[1], wbuf[step % 2, 1, :, columns], preferred_element_type=jnp.float32)
            rounded = total.astype(jnp.bfloat16)
            for b in range(4):
                tok[0, i, b, :, columns] = lax.dot_general(
                    sel[b], rounded[b * CAP : (b + 1) * CAP], contract_slots,
                    preferred_element_type=jnp.float32,
                ).astype(jnp.bfloat16)
            return carry

        lax.fori_loop(0, width // TILE, tile, 0)
        core_copy(i, 1).start()
        core_copy(i, 0).start()

    def combine_cores(i):
        core_copy(i, 1).wait_recv()
        tok[1, i, 0] = (
            tok[0, i, across].astype(jnp.float32) + crecv[i, 1].astype(jnp.float32)
        ).astype(jnp.bfloat16)
        across_copy(i).start()

    def combine_across(i):
        d, s = back[i]
        core_copy(i, 0).wait_recv()
        across_copy(i).wait_recv()
        value = (
            tok[0, i, e].astype(jnp.float32)
            + crecv[i, 0].astype(jnp.float32)
            + xrecv[i].astype(jnp.float32)
        )
        if s:
            tok[1, i, 1] = value.astype(jnp.bfloat16)
            pair_copy(i).start()
            return None
        pair_copy(i - 1).wait_recv()
        value = value + yrecv[d].astype(jnp.float32)
        if d:
            tok[1, i, 2] = value.astype(jnp.bfloat16)
            line_copy(i).start()
            return None
        return value

    value = None
    for i in range(blocks + 2):
        if i < blocks:
            produce(i)
        if 1 <= i <= blocks:
            combine_cores(i - 1)
        if i >= 2:
            value = combine_across(i - 2)
    for i in range(blocks):
        if back[i][1] == 0 and back[i][0]:
            line_copy(i).wait_recv()
            value = value + zrecv[back[i][0] - 1].astype(jnp.float32)

    gain_row = gains[fb_of(0, 0), 0:1, :]
    stream = x_ref[...].astype(jnp.float32)
    scaled = value * gain_row
    share = jnp.sum(scaled * stream, axis=1, keepdims=True)
    tokens = stream.shape[0]
    psend[...] = jnp.broadcast_to(share, (tokens, 128)).T[0:8, :]
    final = []
    for k, peer in enumerate(peers):
        n = 3 + len(peers) + k
        copy = remote(psend, precv.at[k], small_send.at[n], small_recv.at[n], peer)
        copy.start()
        final.append(copy)
    inverse = lax.rsqrt(own_sq[...] / D + epsilon)
    row = psend[...]
    for k, copy in enumerate(final):
        copy.wait_recv()
        row = row + precv[k]
    projection = jnp.broadcast_to(row[0:1, :], (128, tokens)).T[:, 0:1]
    out_ref[...] = (
        inverse * scaled - stream * (inverse * inverse * inverse * projection / D)
    ).astype(out_ref.dtype)
    for copy in final:
        copy.wait_send()
    for i in range(blocks):
        core_copy(i, 0).wait_send()
        core_copy(i, 1).wait_send()
        across_copy(i).wait_send()
        if back[i][1]:
            pair_copy(i).wait_send()
        elif back[i][0]:
            line_copy(i).wait_send()


def fused_shards(residual_stream, grad_output, norm_gain, expert_ids, gate_probs, w_gate, w_up, w_down):
    experts = lax.axis_size("expert")
    T = lax.axis_size("tensor")
    blocks = 2 * T
    tokens, width = residual_stream.shape
    hidden = w_gate.shape[1]
    numbers = jnp.arange(experts, dtype=jnp.int32)
    onehot = (expert_ids[:, :, None] == numbers[None, None, :]).astype(jnp.int32)
    named = onehot.sum(axis=1)
    before = jnp.cumsum(named, axis=0) - named
    slots = jnp.where(named > 0, before, -1).astype(jnp.float32)
    probs = jnp.sum(gate_probs[:, :, None] * onehot.astype(jnp.float32), axis=1)
    meta = jnp.concatenate([slots.T, probs.T], axis=0)
    gain = jnp.broadcast_to(norm_gain.astype(jnp.float32)[None, :], (8, width))
    bf16, f32 = jnp.bfloat16, jnp.float32
    rows = experts * CAP
    vmem = pl.BlockSpec(memory_space=pltpu.VMEM)
    hbm = pl.BlockSpec(memory_space=pl.ANY)
    dma = pltpu.SemaphoreType.DMA
    unit = (tokens, width)
    smalls = 3 + 2 * (blocks - 1)
    return pl.pallas_call(
        functools.partial(fused_kernel, T),
        out_shape=jax.ShapeDtypeStruct(unit, bf16),
        in_specs=[vmem] * 4 + [hbm] * 3,
        out_specs=vmem,
        scratch_shapes=[
            pltpu.VMEM((2, blocks, experts) + unit, bf16),
            pltpu.VMEM((3, hidden // TILE, rows, TILE), f32),
            pltpu.VMEM((2, 3, hidden, width), bf16),
            pltpu.VMEM((2, rows, hidden), bf16),
            pltpu.VMEM((2, rows, width), bf16),
            pltpu.VMEM((blocks, 2) + unit, bf16),
            pltpu.VMEM((blocks,) + unit, bf16),
            pltpu.VMEM((T,) + unit, bf16),
            pltpu.VMEM((T - 1,) + unit, bf16),
            pltpu.VMEM((blocks, 8, width), f32),
            pltpu.VMEM((experts, 8, tokens), f32),
            pltpu.VMEM((experts, CAP, tokens), bf16),
            pltpu.VMEM((rows, 1), f32),
            pltpu.VMEM((rows, 1), f32),
            pltpu.VMEM((tokens, 1), f32),
            pltpu.VMEM((8, tokens), f32),
            pltpu.VMEM((blocks - 1, 8, tokens), f32),
            dma((16 * T,)),
            dma((16 * T,)),
            dma((blocks, 5)),
            dma((blocks, 5)),
            dma((smalls,)),
            dma((smalls,)),
            dma((2, 3)),
            dma((4,)),
        ],
        compiler_params=pltpu.CompilerParams(
            collective_id=0, has_side_effects=True, vmem_limit_bytes=66000000
        ),
        name="fused",
    )(residual_stream, grad_output, gain, meta, w_gate[0], w_up[0], w_down[0])


def solution(mesh):
    placed = (
        P("expert", ("tensor", "kv")),
        P("expert", ("tensor", "kv")),
        P(("tensor", "kv")),
        P("expert", None),
        P("expert", None),
        P("expert", ("tensor", "kv"), None),
        P("expert", ("tensor", "kv"), None),
        P("expert", ("tensor", "kv"), None),
    )
    sizes = dict(mesh.shape)
    width = D // (sizes["tensor"] * sizes["kv"])
    body = fused_shards if sizes["expert"] == 4 and sizes["kv"] == 2 and width % 256 == 0 else shards
    return jax.shard_map(
        body, mesh=mesh, in_specs=placed, out_specs=P("expert", ("tensor", "kv")), check_vma=False
    )
```

```python
import functools

import jax
import jax.numpy as jnp
from jax import lax
from jax.experimental import pallas as pl
from jax.experimental.pallas import tpu as pltpu
from jax.sharding import PartitionSpec as P

D = 4096
CAP = 160


epsilon = 1e-05
contract_width = (((1,), (1,)), ((), ()))
contract_hidden = (((0,), (1,)), ((), ()))
contract_slots = (((0,), (0,)), ((), ()))


def slot_matrix(ids_block, experts):
    flattened = ids_block.reshape(-1)
    onehot = (flattened[:, None] == jnp.arange(experts, dtype=jnp.int32)[None, :]).astype(jnp.int32)
    before = jnp.cumsum(onehot, axis=0) - onehot
    position = jnp.sum(before * onehot, axis=1)
    slot_index = flattened * CAP + position
    table = jnp.arange(experts * CAP, dtype=jnp.int32)
    return (slot_index[None, :] == table[:, None]).astype(jnp.bfloat16)


def shards(residual_stream, grad_output, norm_gain, expert_ids, gate_probs, w_gate, w_up, w_down):
    experts = lax.axis_size("expert")
    local_width = residual_stream.shape[1]
    tokens_here = residual_stream.shape[0]
    stream = residual_stream.astype(jnp.float32)
    squares = lax.psum(jnp.sum(stream * stream, axis=1), ("tensor", "kv"))
    inverse_rms = lax.rsqrt(squares / D + epsilon)[:, None]
    gains = norm_gain.astype(jnp.float32)
    normed = (stream * inverse_rms * gains).astype(jnp.bfloat16)
    table = slot_matrix(expert_ids, experts)
    repeated_x = jnp.repeat(normed, 2, axis=0)
    scaled = (
        jnp.repeat(grad_output.astype(jnp.float32), 2, axis=0) * gate_probs.reshape(-1, 1)
    ).astype(jnp.bfloat16)
    routed_x = jnp.dot(table, repeated_x, preferred_element_type=jnp.float32).astype(jnp.bfloat16)
    routed_grad = jnp.dot(table, scaled, preferred_element_type=jnp.float32).astype(jnp.bfloat16)
    routed_x = routed_x.reshape(experts, CAP, local_width)
    routed_grad = routed_grad.reshape(experts, CAP, local_width)
    gate_weight, up_weight, down_weight = (w_gate[0], w_up[0], w_down[0])
    pieces_x = lax.all_to_all(routed_x, "expert", split_axis=0, concat_axis=0, tiled=True)
    pieces_dy = lax.all_to_all(routed_grad, "expert", split_axis=0, concat_axis=0, tiled=True)
    full_x = lax.all_gather(pieces_x, ("tensor", "kv"), axis=2, tiled=True)
    full_dy = lax.all_gather(pieces_dy, ("tensor", "kv"), axis=2, tiled=True)
    leading = full_x.shape[0]
    items = full_x.shape[1]
    matrix_x = full_x.reshape(leading * items, D)
    matrix_dy = full_dy.reshape(leading * items, D)
    gate_value = lax.dot_general(
        matrix_x, gate_weight, contract_width, preferred_element_type=jnp.float32
    )
    up_value = lax.dot_general(
        matrix_x, up_weight, contract_width, preferred_element_type=jnp.float32
    )
    act_grad = lax.dot_general(
        matrix_dy, down_weight, contract_width, preferred_element_type=jnp.float32
    )
    sigmoid_gate = jax.nn.sigmoid(gate_value)
    activated = gate_value * sigmoid_gate
    gate_grad = (
        act_grad * up_value * sigmoid_gate * (1.0 + gate_value * (1.0 - sigmoid_gate))
    ).astype(jnp.bfloat16)
    up_grad = (act_grad * activated).astype(jnp.bfloat16)
    total = lax.dot_general(
        gate_weight, gate_grad, contract_hidden, preferred_element_type=jnp.float32
    )
    summed = lax.psum_scatter(
        total
        + lax.dot_general(up_weight, up_grad, contract_hidden, preferred_element_type=jnp.float32),
        ("tensor", "kv"),
        scatter_dimension=0,
        tiled=True,
    )
    returned = summed.T.astype(jnp.bfloat16).reshape(leading, items, local_width)
    combined = lax.all_to_all(returned, "expert", split_axis=0, concat_axis=0, tiled=True)
    gathered = lax.dot_general(
        table,
        combined.reshape(experts * CAP, local_width),
        contract_slots,
        preferred_element_type=jnp.float32,
    )
    token_grad = gathered.reshape(tokens_here, 2, local_width).sum(axis=1)
    scaled_grad = token_grad * gains
    projection = lax.psum(jnp.sum(scaled_grad * stream, axis=1), ("tensor", "kv"))[:, None]
    result = inverse_rms * scaled_grad - stream * inverse_rms**3 * projection / D
    return result.astype(jnp.bfloat16)


MESH = pl.DeviceIdType.MESH
TILE = 256


def fused_kernel(
    T, x_ref, dy_ref, gain_ref, meta_ref, wg_ref, wu_ref, wd_ref, out_ref,
    tok, acc, wbuf, hid, routed, crecv, xrecv, yrecv, zrecv, gains, metas, sel, prob,
    ssq, own_sq, psend, precv,
    ag_send, ag_recv, line_send, line_recv, rs_send, rs_recv, small_send, small_recv, wsem, lsem,
):
    e = lax.axis_index("expert")
    z = lax.axis_index("tensor")
    y = lax.axis_index("kv")
    core = e + 1 - 2 * lax.rem(e, 2)
    across = lax.rem(e + 2, 4)
    width = x_ref.shape[1]
    hidden = wg_ref.shape[0]
    tiles = hidden // TILE
    blocks = 2 * T
    inputs = (x_ref, dy_ref)

    def z_of(d):
        return lax.rem(z + T - d, T)

    nearer_low = z < T - 1 - z
    reach = jnp.where(nearer_low, z, T - 1 - z)

    def visit(d):
        if d == 0:
            return z
        near = z + (d + 1) // 2 if d % 2 else z - d // 2
        far = jnp.where(nearer_low, d, T - 1 - d)
        return jnp.where(d <= 2 * reach, near, far)

    def y_of(s):
        return y if s == 0 else 1 - y

    def fb_of(d, s):
        return z_of(d) * 2 + y_of(s)

    def seen(d, s):
        return visit(d) * 2 + y_of(s)

    def b_of(u, c):
        base = core if c else e
        return lax.rem(base + 2 * u, 4)

    def slot(a, d, s, u, c):
        return tok.at[a, seen(d, s), b_of(u, c)]

    def number(a, d, s, u, c):
        return (((a * T + d) * 2 + s) * 2 + u) * 2 + c

    def plan(a, d, s, u, c):
        if c:
            return (d, s, u, 0), (core, z, y)
        if a == 0:
            if u:
                return (d, s, 0, 0), (across, z, y)
            if s:
                return (d, 0, 0, 0), (e, z, 1 - y)
        else:
            if s:
                return (d, 0, u, 0), (e, z, 1 - y)
            if u:
                return (d, 0, 0, 0), (across, z, y)
        raise ValueError(d)

    def gather_copy(a, d, s, u, c):
        source, target = plan(a, d, s, u, c)
        n = number(a, d, s, u, c)
        fb, b = seen(*source[:2]), b_of(*source[2:])
        src = inputs[a] if source == (0, 0, 0, 0) else tok.at[a, fb, b]
        return pltpu.make_async_remote_copy(
            src_ref=src, dst_ref=tok.at[a, fb, b],
            send_sem=ag_send.at[n], recv_sem=ag_recv.at[n],
            device_id=target, device_id_type=MESH,
        )

    def gather_wait(a, d, s, u, c):
        n = number(a, d, s, u, c)
        here = slot(a, d, s, u, c)
        pltpu.make_async_remote_copy(
            src_ref=here, dst_ref=here, send_sem=ag_send.at[n], recv_sem=ag_recv.at[n],
            device_id=plan(a, d, s, u, c)[1], device_id_type=MESH,
        ).wait_recv()

    steps = [(d, s) for d in range(T) for s in (0, 1)]
    back = [(d, s) for d in list(range(1, T)) + [0] for s in (1, 0)]

    def weight_copies(step):
        if step < blocks:
            fb, refs = seen(*steps[step]), (wg_ref, wu_ref, wd_ref)
        else:
            fb, refs = fb_of(*back[step - blocks]), (wg_ref, wu_ref)
        columns = pl.ds(pl.multiple_of(fb * width, width), width)
        return [
            pltpu.make_async_copy(ref.at[:, columns], wbuf.at[step % 2, k], wsem.at[step % 2, k])
            for k, ref in enumerate(refs)
        ]

    for copy in weight_copies(0):
        copy.start()
    local = [
        pltpu.make_async_copy(x_ref, tok.at[0, fb_of(0, 0), e], lsem.at[0]),
        pltpu.make_async_copy(dy_ref, tok.at[1, fb_of(0, 0), e], lsem.at[1]),
        pltpu.make_async_copy(gain_ref, gains.at[fb_of(0, 0)], lsem.at[2]),
        pltpu.make_async_copy(meta_ref, metas.at[e], lsem.at[3]),
    ]
    for copy in local:
        copy.start()

    peers = [(e, lax.rem(z + d, T), y_of(s)) for d in range(T) for s in (0, 1) if d or s]
    sources = [fb_of(d, s) for d in range(T) for s in (0, 1) if d or s]
    others = [(lax.rem(e + k, 4), z, y) for k in (1, 2, 3)]
    barrier = pltpu.get_barrier_semaphore()
    for peer in peers + others:
        pl.semaphore_signal(barrier, inc=1, device_id=peer, device_id_type=MESH)
    pl.semaphore_wait(barrier, len(peers) + len(others))

    def remote(src, dst, send, recv, peer):
        return pltpu.make_async_remote_copy(
            src_ref=src, dst_ref=dst, send_sem=send, recv_sem=recv,
            device_id=peer, device_id_type=MESH,
        )

    small = []
    for k, peer in enumerate(others):
        copy = remote(meta_ref, metas.at[e], small_send.at[k], small_recv.at[k], peer)
        copy.start()
        there = metas.at[lax.rem(e + 3 - k, 4)]
        small.append((copy, remote(there, there, small_send.at[k], small_recv.at[k], peer)))

    def own_line(a, way):
        fb = fb_of(0, 0)
        return remote(
            inputs[a], tok.at[a, fb, e], line_send.at[a, way], line_recv.at[a, z],
            (e, z + 2 * way - 1, y),
        )

    def pass_on(a, d):
        v = visit(d)
        here = tok.at[a, seen(d, 0), e]
        return remote(
            here, here, line_send.at[a, 1 + d], line_recv.at[a, v],
            (e, jnp.where(v < z, z + 1, z - 1), y),
        )

    def passes(d):
        v = visit(d)
        return jnp.where(v < z, z < T - 1, z > 0)

    for a in (0, 1):
        for way in (0, 1):
            @pl.when(z < T - 1 if way else z > 0)
            def _():
                own_line(a, way).start()

    def arrive(a, d):
        pass_on(a, d).wait_recv()

        @pl.when(passes(d))
        def _():
            pass_on(a, d).start()

    for k, peer in enumerate(peers):
        n = 3 + k
        copy = remote(gain_ref, gains.at[fb_of(0, 0)], small_send.at[n], small_recv.at[n], peer)
        copy.start()
        there = gains.at[sources[k]]
        small.append((copy, remote(there, there, small_send.at[n], small_recv.at[n], peer)))

    def level1(d):
        if d:
            arrive(0, d)
        gather_copy(0, d, 1, 0, 0).start()
        if d:
            arrive(1, d)
        gather_copy(1, d, 0, 1, 0).start()
        gather_copy(0, d, 0, 1, 0).start()
        gather_copy(1, d, 1, 0, 0).start()
        gather_copy(0, d, 0, 0, 1).start()
        gather_copy(1, d, 0, 0, 1).start()

    def level2(d):
        gather_wait(0, d, 1, 0, 0)
        gather_copy(0, d, 1, 1, 0).start()
        gather_copy(0, d, 1, 0, 1).start()
        gather_wait(1, d, 0, 1, 0)
        gather_copy(1, d, 1, 1, 0).start()
        gather_copy(1, d, 0, 1, 1).start()

    def level3(d):
        gather_wait(0, d, 0, 1, 0)
        gather_copy(0, d, 0, 1, 1).start()
        gather_wait(1, d, 1, 0, 0)
        gather_copy(1, d, 1, 0, 1).start()
        gather_wait(0, d, 1, 1, 0)
        gather_copy(0, d, 1, 1, 1).start()
        gather_wait(1, d, 1, 1, 0)
        gather_copy(1, d, 1, 1, 1).start()

    def multiply(step):
        d, s = steps[step]
        for copy in weight_copies(step + 1):
            copy.start()
        for a in (0, 1):
            for u in (0, 1):
                gather_wait(a, d, s, u, 1)
        fb = seen(d, s)
        gain_row = gains[fb, 0:1, :]
        mine = tok[0, fb, e].astype(jnp.float32)
        own_sq[...] += jnp.sum(mine * mine, axis=1, keepdims=True)
        for b in range(4):
            rows = pl.ds(b * CAP, CAP)
            picked = jnp.dot(sel[b], tok[0, fb, b], preferred_element_type=jnp.float32)
            ssq[rows, :] += jnp.sum(picked * picked, axis=1, keepdims=True)
            routed[0, rows, :] = (picked * gain_row).astype(jnp.bfloat16)
            picked = jnp.dot(sel[b], tok[1, fb, b], preferred_element_type=jnp.float32)
            routed[1, rows, :] = (picked * prob[rows, :]).astype(jnp.bfloat16)
        for copy in weight_copies(step):
            copy.wait()

        def tile(n, carry):
            rows = pl.ds(pl.multiple_of(n * TILE, TILE), TILE)
            for k in range(3):
                term = lax.dot_general(
                    routed[k // 2], wbuf[step % 2, k, rows, :], contract_width,
                    preferred_element_type=jnp.float32,
                )
                if step == 0:
                    acc[k, n] = term
                else:
                    acc[k, n] += term
            return carry

        lax.fori_loop(0, tiles, tile, 0)

    level1(0)
    level2(0)
    for copy in local:
        copy.wait()
    for copy, arrival in small[:3]:
        arrival.wait_recv()
    own_sq[...] = jnp.zeros_like(own_sq)
    ssq[...] = jnp.zeros_like(ssq)
    for b in range(4):
        slots = metas[b, pl.ds(e, 1), :]
        probs = metas[b, pl.ds(4 + e, 1), :]
        index = lax.broadcasted_iota(jnp.int32, (CAP, slots.shape[1]), 0).astype(jnp.float32)
        chosen = jnp.where(index == slots, 1.0, 0.0)
        sel[b] = chosen.astype(jnp.bfloat16)
        prob[pl.ds(b * CAP, CAP), :] = jnp.sum(chosen * probs, axis=1, keepdims=True)
    for copy, arrival in small[3:]:
        arrival.wait_recv()
    level1(1)
    level3(0)
    multiply(0)
    level2(1)
    level1(2)
    for d in range(3, T):
        level1(d)
    multiply(1)
    level3(1)
    for d in range(2, T):
        multiply(2 * d - 2)
        level2(d)
        multiply(2 * d - 1)
        level3(d)
    multiply(blocks - 2)
    multiply(blocks - 1)
    for a in (0, 1):
        for n in range(1, blocks * 4):
            c, u, s, d = n % 2, n // 2 % 2, n // 4 % 2, n // 8
            if s or u or c:
                gather_copy(a, d, s, u, c).wait_send()
        for way in (0, 1):
            @pl.when(z < T - 1 if way else z > 0)
            def _():
                own_line(a, way).wait_send()
        for d in range(1, T):
            @pl.when(passes(d))
            def _():
                pass_on(a, d).wait_send()
    for copy, arrival in small:
        copy.wait_send()

    inverse = lax.rsqrt(ssq[...] / D + epsilon)

    def activate(n, carry):
        columns = pl.ds(pl.multiple_of(n * TILE, TILE), TILE)
        gate_value = acc[0, n] * inverse
        up_value = acc[1, n] * inverse
        act_grad = acc[2, n]
        sigmoid_gate = jax.nn.sigmoid(gate_value)
        hid[0, :, columns] = (
            act_grad * up_value * sigmoid_gate * (1.0 + gate_value * (1.0 - sigmoid_gate))
        ).astype(jnp.bfloat16)
        hid[1, :, columns] = (act_grad * gate_value * sigmoid_gate).astype(jnp.bfloat16)
        return carry

    lax.fori_loop(0, tiles, activate, 0)

    def core_copy(i, u):
        return remote(
            tok.at[0, i, lax.rem(core + 2 * u, 4)], crecv.at[i, u],
            rs_send.at[i, u], rs_recv.at[i, u], (core, z, y),
        )

    def across_copy(i):
        return remote(tok.at[1, i, 0], xrecv.at[i], rs_send.at[i, 2], rs_recv.at[i, 2], (across, z, y))

    def pair_copy(i):
        d = back[i][0]
        return remote(tok.at[1, i, 1], yrecv.at[d], rs_send.at[i, 3], rs_recv.at[i, 3], (e, z, 1 - y))

    def line_copy(i):
        d = back[i][0]
        return remote(
            tok.at[1, i, 2], zrecv.at[d - 1], rs_send.at[i, 4], rs_recv.at[i, 4], (e, z_of(d), y)
        )

    def produce(i):
        step = blocks + i
        if i + 1 < blocks:
            for copy in weight_copies(step + 1):
                copy.start()
        for copy in weight_copies(step):
            copy.wait()

        def tile(n, carry):
            columns = pl.ds(pl.multiple_of(n * TILE, TILE), TILE)
            total = jnp.dot(
                hid[0], wbuf[step % 2, 0, :, columns], preferred_element_type=jnp.float32
            ) + jnp.dot(hid[1], wbuf[step % 2, 1, :, columns], preferred_element_type=jnp.float32)
            rounded = total.astype(jnp.bfloat16)
            for b in range(4):
                tok[0, i, b, :, columns] = lax.dot_general(
                    sel[b], rounded[b * CAP : (b + 1) * CAP], contract_slots,
                    preferred_element_type=jnp.float32,
                ).astype(jnp.bfloat16)
            return carry

        lax.fori_loop(0, width // TILE, tile, 0)
        core_copy(i, 1).start()
        core_copy(i, 0).start()

    def combine_cores(i):
        core_copy(i, 1).wait_recv()
        tok[1, i, 0] = (
            tok[0, i, across].astype(jnp.float32) + crecv[i, 1].astype(jnp.float32)
        ).astype(jnp.bfloat16)
        across_copy(i).start()

    def combine_across(i):
        d, s = back[i]
        core_copy(i, 0).wait_recv()
        across_copy(i).wait_recv()
        value = (
            tok[0, i, e].astype(jnp.float32)
            + crecv[i, 0].astype(jnp.float32)
            + xrecv[i].astype(jnp.float32)
        )
        if s:
            tok[1, i, 1] = value.astype(jnp.bfloat16)
            pair_copy(i).start()
            return None
        pair_copy(i - 1).wait_recv()
        value = value + yrecv[d].astype(jnp.float32)
        if d:
            tok[1, i, 2] = value.astype(jnp.bfloat16)
            line_copy(i).start()
            return None
        return value

    value = None
    for i in range(blocks + 2):
        if i < blocks:
            produce(i)
        if 1 <= i <= blocks:
            combine_cores(i - 1)
        if i >= 2:
            value = combine_across(i - 2)
    for i in range(blocks):
        if back[i][1] == 0 and back[i][0]:
            line_copy(i).wait_recv()
            value = value + zrecv[back[i][0] - 1].astype(jnp.float32)

    gain_row = gains[fb_of(0, 0), 0:1, :]
    stream = x_ref[...].astype(jnp.float32)
    scaled = value * gain_row
    share = jnp.sum(scaled * stream, axis=1, keepdims=True)
    tokens = stream.shape[0]
    psend[...] = jnp.broadcast_to(share, (tokens, 128)).T[0:8, :]
    final = []
    for k, peer in enumerate(peers):
        n = 3 + len(peers) + k
        copy = remote(psend, precv.at[k], small_send.at[n], small_recv.at[n], peer)
        copy.start()
        final.append(copy)
    inverse = lax.rsqrt(own_sq[...] / D + epsilon)
    row = psend[...]
    for k, copy in enumerate(final):
        copy.wait_recv()
        row = row + precv[k]
    projection = jnp.broadcast_to(row[0:1, :], (128, tokens)).T[:, 0:1]
    out_ref[...] = (
        inverse * scaled - stream * (inverse * inverse * inverse * projection / D)
    ).astype(out_ref.dtype)
    for copy in final:
        copy.wait_send()
    for i in range(blocks):
        core_copy(i, 0).wait_send()
        core_copy(i, 1).wait_send()
        across_copy(i).wait_send()
        if back[i][1]:
            pair_copy(i).wait_send()
        elif back[i][0]:
            line_copy(i).wait_send()


def fused_shards(residual_stream, grad_output, norm_gain, expert_ids, gate_probs, w_gate, w_up, w_down):
    experts = lax.axis_size("expert")
    T = lax.axis_size("tensor")
    blocks = 2 * T
    tokens, width = residual_stream.shape
    hidden = w_gate.shape[1]
    numbers = jnp.arange(experts, dtype=jnp.int32)
    onehot = (expert_ids[:, :, None] == numbers[None, None, :]).astype(jnp.int32)
    named = onehot.sum(axis=1)
    before = jnp.cumsum(named, axis=0) - named
    slots = jnp.where(named > 0, before, -1).astype(jnp.float32)
    probs = jnp.sum(gate_probs[:, :, None] * onehot.astype(jnp.float32), axis=1)
    meta = jnp.concatenate([slots.T, probs.T], axis=0)
    gain = jnp.broadcast_to(norm_gain.astype(jnp.float32)[None, :], (8, width))
    bf16, f32 = jnp.bfloat16, jnp.float32
    rows = experts * CAP
    vmem = pl.BlockSpec(memory_space=pltpu.VMEM)
    hbm = pl.BlockSpec(memory_space=pl.ANY)
    dma = pltpu.SemaphoreType.DMA
    unit = (tokens, width)
    smalls = 3 + 2 * (blocks - 1)
    return pl.pallas_call(
        functools.partial(fused_kernel, T),
        out_shape=jax.ShapeDtypeStruct(unit, bf16),
        in_specs=[vmem] * 4 + [hbm] * 3,
        out_specs=vmem,
        scratch_shapes=[
            pltpu.VMEM((2, blocks, experts) + unit, bf16),
            pltpu.VMEM((3, hidden // TILE, rows, TILE), f32),
            pltpu.VMEM((2, 3, hidden, width), bf16),
            pltpu.VMEM((2, rows, hidden), bf16),
            pltpu.VMEM((2, rows, width), bf16),
            pltpu.VMEM((blocks, 2) + unit, bf16),
            pltpu.VMEM((blocks,) + unit, bf16),
            pltpu.VMEM((T,) + unit, bf16),
            pltpu.VMEM((T - 1,) + unit, bf16),
            pltpu.VMEM((blocks, 8, width), f32),
            pltpu.VMEM((experts, 8, tokens), f32),
            pltpu.VMEM((experts, CAP, tokens), bf16),
            pltpu.VMEM((rows, 1), f32),
            pltpu.VMEM((rows, 1), f32),
            pltpu.VMEM((tokens, 1), f32),
            pltpu.VMEM((8, tokens), f32),
            pltpu.VMEM((blocks - 1, 8, tokens), f32),
            dma((16 * T,)),
            dma((16 * T,)),
            dma((2, T + 1)),
            dma((2, T)),
            dma((blocks, 5)),
            dma((blocks, 5)),
            dma((smalls,)),
            dma((smalls,)),
            dma((2, 3)),
            dma((4,)),
        ],
        compiler_params=pltpu.CompilerParams(
            collective_id=0, has_side_effects=True, vmem_limit_bytes=66000000
        ),
        name="fused",
    )(residual_stream, grad_output, gain, meta, w_gate[0], w_up[0], w_down[0])


def solution(mesh):
    placed = (
        P("expert", ("tensor", "kv")),
        P("expert", ("tensor", "kv")),
        P(("tensor", "kv")),
        P("expert", None),
        P("expert", None),
        P("expert", ("tensor", "kv"), None),
        P("expert", ("tensor", "kv"), None),
        P("expert", ("tensor", "kv"), None),
    )
    sizes = dict(mesh.shape)
    width = D // (sizes["tensor"] * sizes["kv"])
    body = fused_shards if sizes["expert"] == 4 and sizes["kv"] == 2 and width % 256 == 0 else shards
    return jax.shard_map(
        body, mesh=mesh, in_specs=placed, out_specs=P("expert", ("tensor", "kv")), check_vma=False
    )
```

```python
import functools

import jax
import jax.numpy as jnp
from jax import lax
from jax.experimental import pallas as pl
from jax.experimental.pallas import tpu as pltpu
from jax.sharding import PartitionSpec as P

D = 4096
CAP = 160


epsilon = 1e-05
contract_width = (((1,), (1,)), ((), ()))
contract_hidden = (((0,), (1,)), ((), ()))
contract_slots = (((0,), (0,)), ((), ()))


def slot_matrix(ids_block, experts):
    flattened = ids_block.reshape(-1)
    onehot = (flattened[:, None] == jnp.arange(experts, dtype=jnp.int32)[None, :]).astype(jnp.int32)
    before = jnp.cumsum(onehot, axis=0) - onehot
    position = jnp.sum(before * onehot, axis=1)
    slot_index = flattened * CAP + position
    table = jnp.arange(experts * CAP, dtype=jnp.int32)
    return (slot_index[None, :] == table[:, None]).astype(jnp.bfloat16)


def shards(residual_stream, grad_output, norm_gain, expert_ids, gate_probs, w_gate, w_up, w_down):
    experts = lax.axis_size("expert")
    local_width = residual_stream.shape[1]
    tokens_here = residual_stream.shape[0]
    stream = residual_stream.astype(jnp.float32)
    squares = lax.psum(jnp.sum(stream * stream, axis=1), ("tensor", "kv"))
    inverse_rms = lax.rsqrt(squares / D + epsilon)[:, None]
    gains = norm_gain.astype(jnp.float32)
    normed = (stream * inverse_rms * gains).astype(jnp.bfloat16)
    table = slot_matrix(expert_ids, experts)
    repeated_x = jnp.repeat(normed, 2, axis=0)
    scaled = (
        jnp.repeat(grad_output.astype(jnp.float32), 2, axis=0) * gate_probs.reshape(-1, 1)
    ).astype(jnp.bfloat16)
    routed_x = jnp.dot(table, repeated_x, preferred_element_type=jnp.float32).astype(jnp.bfloat16)
    routed_grad = jnp.dot(table, scaled, preferred_element_type=jnp.float32).astype(jnp.bfloat16)
    routed_x = routed_x.reshape(experts, CAP, local_width)
    routed_grad = routed_grad.reshape(experts, CAP, local_width)
    gate_weight, up_weight, down_weight = (w_gate[0], w_up[0], w_down[0])
    pieces_x = lax.all_to_all(routed_x, "expert", split_axis=0, concat_axis=0, tiled=True)
    pieces_dy = lax.all_to_all(routed_grad, "expert", split_axis=0, concat_axis=0, tiled=True)
    full_x = lax.all_gather(pieces_x, ("tensor", "kv"), axis=2, tiled=True)
    full_dy = lax.all_gather(pieces_dy, ("tensor", "kv"), axis=2, tiled=True)
    leading = full_x.shape[0]
    items = full_x.shape[1]
    matrix_x = full_x.reshape(leading * items, D)
    matrix_dy = full_dy.reshape(leading * items, D)
    gate_value = lax.dot_general(
        matrix_x, gate_weight, contract_width, preferred_element_type=jnp.float32
    )
    up_value = lax.dot_general(
        matrix_x, up_weight, contract_width, preferred_element_type=jnp.float32
    )
    act_grad = lax.dot_general(
        matrix_dy, down_weight, contract_width, preferred_element_type=jnp.float32
    )
    sigmoid_gate = jax.nn.sigmoid(gate_value)
    activated = gate_value * sigmoid_gate
    gate_grad = (
        act_grad * up_value * sigmoid_gate * (1.0 + gate_value * (1.0 - sigmoid_gate))
    ).astype(jnp.bfloat16)
    up_grad = (act_grad * activated).astype(jnp.bfloat16)
    total = lax.dot_general(
        gate_weight, gate_grad, contract_hidden, preferred_element_type=jnp.float32
    )
    summed = lax.psum_scatter(
        total
        + lax.dot_general(up_weight, up_grad, contract_hidden, preferred_element_type=jnp.float32),
        ("tensor", "kv"),
        scatter_dimension=0,
        tiled=True,
    )
    returned = summed.T.astype(jnp.bfloat16).reshape(leading, items, local_width)
    combined = lax.all_to_all(returned, "expert", split_axis=0, concat_axis=0, tiled=True)
    gathered = lax.dot_general(
        table,
        combined.reshape(experts * CAP, local_width),
        contract_slots,
        preferred_element_type=jnp.float32,
    )
    token_grad = gathered.reshape(tokens_here, 2, local_width).sum(axis=1)
    scaled_grad = token_grad * gains
    projection = lax.psum(jnp.sum(scaled_grad * stream, axis=1), ("tensor", "kv"))[:, None]
    result = inverse_rms * scaled_grad - stream * inverse_rms**3 * projection / D
    return result.astype(jnp.bfloat16)


MESH = pl.DeviceIdType.MESH
TILE = 256


def fused_kernel(
    T, x_ref, dy_ref, gain_ref, meta_ref, wg_ref, wu_ref, wd_ref, out_ref,
    tok, acc, wbuf, hid, routed, crecv, xrecv, yrecv, zrecv, gains, metas, sel, prob,
    ssq, own_sq, psend, precv,
    ag_send, ag_recv, line_send, line_recv, rs_send, rs_recv, small_send, small_recv, wsem, lsem,
):
    e = lax.axis_index("expert")
    z = lax.axis_index("tensor")
    y = lax.axis_index("kv")
    core = e + 1 - 2 * lax.rem(e, 2)
    across = lax.rem(e + 2, 4)
    width = x_ref.shape[1]
    hidden = wg_ref.shape[0]
    tiles = hidden // TILE
    blocks = 2 * T
    inputs = (x_ref, dy_ref)

    def z_of(d):
        return lax.rem(z + T - d, T)

    nearer_low = z < T - 1 - z
    reach = jnp.where(nearer_low, z, T - 1 - z)

    def visit(d):
        if d == 0:
            return z
        near = z + (d + 1) // 2 if d % 2 else z - d // 2
        far = jnp.where(nearer_low, d, T - 1 - d)
        return jnp.where(d <= 2 * reach, near, far)

    def y_of(s):
        return y if s == 0 else 1 - y

    def fb_of(d, s):
        return z_of(d) * 2 + y_of(s)

    def seen(d, s):
        return visit(d) * 2 + y_of(s)

    def b_of(u, c):
        base = core if c else e
        return lax.rem(base + 2 * u, 4)

    def slot(a, d, s, u, c):
        return tok.at[a, seen(d, s), b_of(u, c)]

    def number(a, d, s, u, c):
        return (((a * T + d) * 2 + s) * 2 + u) * 2 + c

    def plan(a, d, s, u, c):
        if c:
            return (d, s, u, 0), (core, z, y)
        if a == 0:
            if u:
                return (d, s, 0, 0), (across, z, y)
            if s:
                return (d, 0, 0, 0), (e, z, 1 - y)
        else:
            if s:
                return (d, 0, u, 0), (e, z, 1 - y)
            if u:
                return (d, 0, 0, 0), (across, z, y)
        raise ValueError(d)

    def gather_copy(a, d, s, u, c):
        source, target = plan(a, d, s, u, c)
        n = number(a, d, s, u, c)
        fb, b = seen(*source[:2]), b_of(*source[2:])
        src = inputs[a] if source == (0, 0, 0, 0) else tok.at[a, fb, b]
        return pltpu.make_async_remote_copy(
            src_ref=src, dst_ref=tok.at[a, fb, b],
            send_sem=ag_send.at[n], recv_sem=ag_recv.at[n],
            device_id=target, device_id_type=MESH,
        )

    def gather_wait(a, d, s, u, c):
        n = number(a, d, s, u, c)
        here = slot(a, d, s, u, c)
        pltpu.make_async_remote_copy(
            src_ref=here, dst_ref=here, send_sem=ag_send.at[n], recv_sem=ag_recv.at[n],
            device_id=plan(a, d, s, u, c)[1], device_id_type=MESH,
        ).wait_recv()

    steps = [(d, s) for d in range(T) for s in (0, 1)]
    back = [(d, s) for d in list(range(1, T)) + [0] for s in (1, 0)]

    def weight_copies(step):
        if step < blocks:
            fb, refs = seen(*steps[step]), (wg_ref, wu_ref, wd_ref)
        else:
            fb, refs = fb_of(*back[step - blocks]), (wg_ref, wu_ref)
        columns = pl.ds(pl.multiple_of(fb * width, width), width)
        return [
            pltpu.make_async_copy(ref.at[:, columns], wbuf.at[step % 2, k], wsem.at[step % 2, k])
            for k, ref in enumerate(refs)
        ]

    for copy in weight_copies(0):
        copy.start()
    local = [
        pltpu.make_async_copy(x_ref, tok.at[0, fb_of(0, 0), e], lsem.at[0]),
        pltpu.make_async_copy(dy_ref, tok.at[1, fb_of(0, 0), e], lsem.at[1]),
        pltpu.make_async_copy(gain_ref, gains.at[fb_of(0, 0)], lsem.at[2]),
        pltpu.make_async_copy(meta_ref, metas.at[e], lsem.at[3]),
    ]
    for copy in local:
        copy.start()

    peers = [(e, lax.rem(z + d, T), y_of(s)) for d in range(T) for s in (0, 1) if d or s]
    sources = [fb_of(d, s) for d in range(T) for s in (0, 1) if d or s]
    others = [(lax.rem(e + k, 4), z, y) for k in (1, 2, 3)]
    barrier = pltpu.get_barrier_semaphore()
    for peer in peers + others:
        pl.semaphore_signal(barrier, inc=1, device_id=peer, device_id_type=MESH)
    pl.semaphore_wait(barrier, len(peers) + len(others))

    def remote(src, dst, send, recv, peer):
        return pltpu.make_async_remote_copy(
            src_ref=src, dst_ref=dst, send_sem=send, recv_sem=recv,
            device_id=peer, device_id_type=MESH,
        )

    small = []
    for k, peer in enumerate(others):
        copy = remote(meta_ref, metas.at[e], small_send.at[k], small_recv.at[k], peer)
        copy.start()
        there = metas.at[lax.rem(e + 3 - k, 4)]
        small.append((copy, remote(there, there, small_send.at[k], small_recv.at[k], peer)))

    def own_line(a, way):
        fb = fb_of(0, 0)
        return remote(
            inputs[a], tok.at[a, fb, e], line_send.at[a, way], line_recv.at[a, z],
            (e, z + 2 * way - 1, y),
        )

    def pass_on(a, d):
        v = visit(d)
        here = tok.at[a, seen(d, 0), e]
        return remote(
            here, here, line_send.at[a, 1 + d], line_recv.at[a, v],
            (e, jnp.where(v < z, z + 1, z - 1), y),
        )

    def passes(d):
        v = visit(d)
        return jnp.where(v < z, z < T - 1, z > 0)

    for a in (0, 1):
        for way in (0, 1):
            @pl.when(z < T - 1 if way else z > 0)
            def _():
                own_line(a, way).start()

    def arrive(a, d):
        pass_on(a, d).wait_recv()

        @pl.when(passes(d))
        def _():
            pass_on(a, d).start()

    for k, peer in enumerate(peers):
        n = 3 + k
        copy = remote(gain_ref, gains.at[fb_of(0, 0)], small_send.at[n], small_recv.at[n], peer)
        copy.start()
        there = gains.at[sources[k]]
        small.append((copy, remote(there, there, small_send.at[n], small_recv.at[n], peer)))

    def level1(d):
        if d:
            arrive(0, d)
        gather_copy(0, d, 1, 0, 0).start()
        if d:
            arrive(1, d)
        gather_copy(1, d, 0, 1, 0).start()
        gather_copy(0, d, 0, 1, 0).start()
        gather_copy(1, d, 1, 0, 0).start()
        gather_copy(0, d, 0, 0, 1).start()
        gather_copy(1, d, 0, 0, 1).start()

    def level2(d):
        gather_wait(0, d, 1, 0, 0)
        gather_copy(0, d, 1, 1, 0).start()
        gather_copy(0, d, 1, 0, 1).start()
        gather_wait(1, d, 0, 1, 0)
        gather_copy(1, d, 1, 1, 0).start()
        gather_copy(1, d, 0, 1, 1).start()

    def level3(d):
        gather_wait(0, d, 0, 1, 0)
        gather_copy(0, d, 0, 1, 1).start()
        gather_wait(1, d, 1, 0, 0)
        gather_copy(1, d, 1, 0, 1).start()
        gather_wait(0, d, 1, 1, 0)
        gather_copy(0, d, 1, 1, 1).start()
        gather_wait(1, d, 1, 1, 0)
        gather_copy(1, d, 1, 1, 1).start()

    def multiply(step):
        d, s = steps[step]
        for copy in weight_copies(step + 1):
            copy.start()
        for a in (0, 1):
            for u in (0, 1):
                gather_wait(a, d, s, u, 1)
        fb = seen(d, s)
        gain_row = gains[fb, 0:1, :]
        mine = tok[0, fb, e].astype(jnp.float32)
        own_sq[...] += jnp.sum(mine * mine, axis=1, keepdims=True)
        for b in range(4):
            rows = pl.ds(b * CAP, CAP)
            picked = jnp.dot(sel[b], tok[0, fb, b], preferred_element_type=jnp.float32)
            ssq[rows, :] += jnp.sum(picked * picked, axis=1, keepdims=True)
            routed[0, rows, :] = (picked * gain_row).astype(jnp.bfloat16)
            picked = jnp.dot(sel[b], tok[1, fb, b], preferred_element_type=jnp.float32)
            routed[1, rows, :] = (picked * prob[rows, :]).astype(jnp.bfloat16)
        for copy in weight_copies(step):
            copy.wait()

        def tile(n, carry):
            rows = pl.ds(pl.multiple_of(n * TILE, TILE), TILE)
            for k in range(3):
                term = lax.dot_general(
                    routed[k // 2], wbuf[step % 2, k, rows, :], contract_width,
                    preferred_element_type=jnp.float32,
                )
                if step == 0:
                    acc[k, n] = term
                else:
                    acc[k, n] += term
            return carry

        lax.fori_loop(0, tiles, tile, 0)

    level1(0)
    level2(0)
    for copy in local:
        copy.wait()
    for copy, arrival in small[:3]:
        arrival.wait_recv()
    own_sq[...] = jnp.zeros_like(own_sq)
    ssq[...] = jnp.zeros_like(ssq)
    for b in range(4):
        slots = metas[b, pl.ds(e, 1), :]
        probs = metas[b, pl.ds(4 + e, 1), :]
        index = lax.broadcasted_iota(jnp.int32, (CAP, slots.shape[1]), 0).astype(jnp.float32)
        chosen = jnp.where(index == slots, 1.0, 0.0)
        sel[b] = chosen.astype(jnp.bfloat16)
        prob[pl.ds(b * CAP, CAP), :] = jnp.sum(chosen * probs, axis=1, keepdims=True)
    for copy, arrival in small[3:]:
        arrival.wait_recv()
    level1(1)
    level3(0)
    multiply(0)
    level2(1)
    level1(2)
    for d in range(3, T):
        level1(d)
    multiply(1)
    level3(1)
    for d in range(2, T):
        if d == 2:
            level2(d)
            multiply(2 * d - 2)
        else:
            multiply(2 * d - 2)
            level2(d)
        multiply(2 * d - 1)
        level3(d)
    multiply(blocks - 2)
    multiply(blocks - 1)
    for a in (0, 1):
        for n in range(1, blocks * 4):
            c, u, s, d = n % 2, n // 2 % 2, n // 4 % 2, n // 8
            if s or u or c:
                gather_copy(a, d, s, u, c).wait_send()
        for way in (0, 1):
            @pl.when(z < T - 1 if way else z > 0)
            def _():
                own_line(a, way).wait_send()
        for d in range(1, T):
            @pl.when(passes(d))
            def _():
                pass_on(a, d).wait_send()
    for copy, arrival in small:
        copy.wait_send()

    inverse = lax.rsqrt(ssq[...] / D + epsilon)

    def activate(n, carry):
        columns = pl.ds(pl.multiple_of(n * TILE, TILE), TILE)
        gate_value = acc[0, n] * inverse
        up_value = acc[1, n] * inverse
        act_grad = acc[2, n]
        sigmoid_gate = jax.nn.sigmoid(gate_value)
        hid[0, :, columns] = (
            act_grad * up_value * sigmoid_gate * (1.0 + gate_value * (1.0 - sigmoid_gate))
        ).astype(jnp.bfloat16)
        hid[1, :, columns] = (act_grad * gate_value * sigmoid_gate).astype(jnp.bfloat16)
        return carry

    lax.fori_loop(0, tiles, activate, 0)

    def core_copy(i, u):
        return remote(
            tok.at[0, i, lax.rem(core + 2 * u, 4)], crecv.at[i, u],
            rs_send.at[i, u], rs_recv.at[i, u], (core, z, y),
        )

    def across_copy(i):
        return remote(tok.at[1, i, 0], xrecv.at[i], rs_send.at[i, 2], rs_recv.at[i, 2], (across, z, y))

    def pair_copy(i):
        d = back[i][0]
        return remote(tok.at[1, i, 1], yrecv.at[d], rs_send.at[i, 3], rs_recv.at[i, 3], (e, z, 1 - y))

    def line_copy(i):
        d = back[i][0]
        return remote(
            tok.at[1, i, 2], zrecv.at[d - 1], rs_send.at[i, 4], rs_recv.at[i, 4], (e, z_of(d), y)
        )

    def produce(i):
        step = blocks + i
        if i + 1 < blocks:
            for copy in weight_copies(step + 1):
                copy.start()
        for copy in weight_copies(step):
            copy.wait()

        def tile(n, carry):
            columns = pl.ds(pl.multiple_of(n * TILE, TILE), TILE)
            total = jnp.dot(
                hid[0], wbuf[step % 2, 0, :, columns], preferred_element_type=jnp.float32
            ) + jnp.dot(hid[1], wbuf[step % 2, 1, :, columns], preferred_element_type=jnp.float32)
            rounded = total.astype(jnp.bfloat16)
            for b in range(4):
                tok[0, i, b, :, columns] = lax.dot_general(
                    sel[b], rounded[b * CAP : (b + 1) * CAP], contract_slots,
                    preferred_element_type=jnp.float32,
                ).astype(jnp.bfloat16)
            return carry

        lax.fori_loop(0, width // TILE, tile, 0)
        core_copy(i, 1).start()
        core_copy(i, 0).start()

    def combine_cores(i):
        core_copy(i, 1).wait_recv()
        tok[1, i, 0] = (
            tok[0, i, across].astype(jnp.float32) + crecv[i, 1].astype(jnp.float32)
        ).astype(jnp.bfloat16)
        across_copy(i).start()

    def combine_across(i):
        d, s = back[i]
        core_copy(i, 0).wait_recv()
        across_copy(i).wait_recv()
        value = (
            tok[0, i, e].astype(jnp.float32)
            + crecv[i, 0].astype(jnp.float32)
            + xrecv[i].astype(jnp.float32)
        )
        if s:
            tok[1, i, 1] = value.astype(jnp.bfloat16)
            pair_copy(i).start()
            return None
        pair_copy(i - 1).wait_recv()
        value = value + yrecv[d].astype(jnp.float32)
        if d:
            tok[1, i, 2] = value.astype(jnp.bfloat16)
            line_copy(i).start()
            return None
        return value

    value = None
    for i in range(blocks + 2):
        if i < blocks:
            produce(i)
        if 1 <= i <= blocks:
            combine_cores(i - 1)
        if i >= 2:
            value = combine_across(i - 2)
    for i in range(blocks):
        if back[i][1] == 0 and back[i][0]:
            line_copy(i).wait_recv()
            value = value + zrecv[back[i][0] - 1].astype(jnp.float32)

    gain_row = gains[fb_of(0, 0), 0:1, :]
    stream = x_ref[...].astype(jnp.float32)
    scaled = value * gain_row
    share = jnp.sum(scaled * stream, axis=1, keepdims=True)
    tokens = stream.shape[0]
    psend[...] = jnp.broadcast_to(share, (tokens, 128)).T[0:8, :]
    final = []
    for k, peer in enumerate(peers):
        n = 3 + len(peers) + k
        copy = remote(psend, precv.at[k], small_send.at[n], small_recv.at[n], peer)
        copy.start()
        final.append(copy)
    inverse = lax.rsqrt(own_sq[...] / D + epsilon)
    row = psend[...]
    for k, copy in enumerate(final):
        copy.wait_recv()
        row = row + precv[k]
    projection = jnp.broadcast_to(row[0:1, :], (128, tokens)).T[:, 0:1]
    out_ref[...] = (
        inverse * scaled - stream * (inverse * inverse * inverse * projection / D)
    ).astype(out_ref.dtype)
    for copy in final:
        copy.wait_send()
    for i in range(blocks):
        core_copy(i, 0).wait_send()
        core_copy(i, 1).wait_send()
        across_copy(i).wait_send()
        if back[i][1]:
            pair_copy(i).wait_send()
        elif back[i][0]:
            line_copy(i).wait_send()


def fused_shards(residual_stream, grad_output, norm_gain, expert_ids, gate_probs, w_gate, w_up, w_down):
    experts = lax.axis_size("expert")
    T = lax.axis_size("tensor")
    blocks = 2 * T
    tokens, width = residual_stream.shape
    hidden = w_gate.shape[1]
    numbers = jnp.arange(experts, dtype=jnp.int32)
    onehot = (expert_ids[:, :, None] == numbers[None, None, :]).astype(jnp.int32)
    named = onehot.sum(axis=1)
    before = jnp.cumsum(named, axis=0) - named
    slots = jnp.where(named > 0, before, -1).astype(jnp.float32)
    probs = jnp.sum(gate_probs[:, :, None] * onehot.astype(jnp.float32), axis=1)
    meta = jnp.concatenate([slots.T, probs.T], axis=0)
    gain = jnp.broadcast_to(norm_gain.astype(jnp.float32)[None, :], (8, width))
    bf16, f32 = jnp.bfloat16, jnp.float32
    rows = experts * CAP
    vmem = pl.BlockSpec(memory_space=pltpu.VMEM)
    hbm = pl.BlockSpec(memory_space=pl.ANY)
    dma = pltpu.SemaphoreType.DMA
    unit = (tokens, width)
    smalls = 3 + 2 * (blocks - 1)
    return pl.pallas_call(
        functools.partial(fused_kernel, T),
        out_shape=jax.ShapeDtypeStruct(unit, bf16),
        in_specs=[vmem] * 4 + [hbm] * 3,
        out_specs=vmem,
        scratch_shapes=[
            pltpu.VMEM((2, blocks, experts) + unit, bf16),
            pltpu.VMEM((3, hidden // TILE, rows, TILE), f32),
            pltpu.VMEM((2, 3, hidden, width), bf16),
            pltpu.VMEM((2, rows, hidden), bf16),
            pltpu.VMEM((2, rows, width), bf16),
            pltpu.VMEM((blocks, 2) + unit, bf16),
            pltpu.VMEM((blocks,) + unit, bf16),
            pltpu.VMEM((T,) + unit, bf16),
            pltpu.VMEM((T - 1,) + unit, bf16),
            pltpu.VMEM((blocks, 8, width), f32),
            pltpu.VMEM((experts, 8, tokens), f32),
            pltpu.VMEM((experts, CAP, tokens), bf16),
            pltpu.VMEM((rows, 1), f32),
            pltpu.VMEM((rows, 1), f32),
            pltpu.VMEM((tokens, 1), f32),
            pltpu.VMEM((8, tokens), f32),
            pltpu.VMEM((blocks - 1, 8, tokens), f32),
            dma((16 * T,)),
            dma((16 * T,)),
            dma((2, T + 1)),
            dma((2, T)),
            dma((blocks, 5)),
            dma((blocks, 5)),
            dma((smalls,)),
            dma((smalls,)),
            dma((2, 3)),
            dma((4,)),
        ],
        compiler_params=pltpu.CompilerParams(
            collective_id=0, has_side_effects=True, vmem_limit_bytes=66000000
        ),
        name="fused",
    )(residual_stream, grad_output, gain, meta, w_gate[0], w_up[0], w_down[0])


def solution(mesh):
    placed = (
        P("expert", ("tensor", "kv")),
        P("expert", ("tensor", "kv")),
        P(("tensor", "kv")),
        P("expert", None),
        P("expert", None),
        P("expert", ("tensor", "kv"), None),
        P("expert", ("tensor", "kv"), None),
        P("expert", ("tensor", "kv"), None),
    )
    sizes = dict(mesh.shape)
    width = D // (sizes["tensor"] * sizes["kv"])
    body = fused_shards if sizes["expert"] == 4 and sizes["kv"] == 2 and width % 256 == 0 else shards
    return jax.shard_map(
        body, mesh=mesh, in_specs=placed, out_specs=P("expert", ("tensor", "kv")), check_vma=False
    )
```
